512 devices in a mesh: dp: 64 (over x, z_lo, core), tensor: 8 (over z_hi, y).
Axes of the slice: x: 4, y: 4, z: 16 (z_hi: 2, z_lo: 8; z = z_hi * 8 + z_lo), core: 2. Of those that a mesh axis runs over, the one named last changes fastest.
Arguments:
- tokens: bfloat16 [16384, 3072], P('dp', 'tensor'), may hold values from -6 to 6
- expert_ids: int32 [16384, 2], P('dp'), may hold values from 0 to 7, as said below
- combine_weights: float32 [16384, 2], P('dp'), may hold values from 0.1 to 1
- grad_out: bfloat16 [16384, 3072], P('dp', 'tensor'), may hold values from -6 to 6
- gate_pre: bfloat16 [8192, 8192], P('dp', 'tensor'), may hold values from -6 to 6
- w_up: bfloat16 [3072, 8192], P('dp', 'tensor'), may hold values from -0.109375 to 0.109375
- w_down: bfloat16 [3072, 8192], P('dp', 'tensor'), may hold values from -0.0625 to 0.0625
Outputs:
- mixed: bfloat16 [16384, 3072], P('dp', 'tensor')
- grad_tokens: bfloat16 [16384, 3072], P('dp', 'tensor')
- grad_gate: bfloat16 [8192, 8192], P('dp', 'tensor')
The draws below stay inside these ranges and needn't reach their ends.
Inputs may be any that keep to these rules, and one draw needn't show every extreme that they name: `expert_ids`: each row names two different experts. In every aligned block of 256 rows at most 128 rows name expert 0, and in some block exactly 128. Rows of gate_pre in empty slots are not read.
All inputs are finite; a program needn't handle non-finite values.
Results may differ from the reference program's by a relative error of at most 0.014.
Values may be sent and summed in bfloat16 or wider, within the bound.
No kernel may reach another device: no remote copies, remote signals or barrier semaphores. Data moves between devices by JAX's collectives and lax.ppermute only.
A program may use at most 64 MiB of HBM per device.

```python
import jax
import jax.numpy as jnp
from jax import lax

D = 3072
FF = 8192
EXPERTS = 8
CAP = 128
TOK_DEV = 256
TOKENS = 16384
SLOTS = 8192
N_DP = 64
N_TENSOR = 8


def draw_expert_ids(key, part):
    subkeys = jax.random.split(key, 6)
    load_counts = jax.random.randint(subkeys[0], (N_DP,), 0, CAP + 1)
    fullest = jax.random.randint(subkeys[1], (), 0, N_DP)
    load_counts = jnp.where(jnp.arange(N_DP) == fullest, CAP, load_counts)

    def one_order(order_key):
        return jax.random.permutation(order_key, TOK_DEV)
    orders = jax.vmap(one_order)(jax.random.split(subkeys[2], N_DP))
    routed = orders < load_counts[:, None]
    other_id = jax.random.randint(subkeys[3], (N_DP, TOK_DEV), 1, EXPERTS)
    offset = jax.random.randint(subkeys[4], (N_DP, TOK_DEV), 1, EXPERTS - 1)
    second = 1 + (other_id - 1 + offset) % (EXPERTS - 1)
    column = jax.random.randint(subkeys[5], (N_DP, TOK_DEV), 0, 2)
    first_id = jnp.where(routed & (column == 0), 0, other_id)
    second_id = jnp.where(routed, jnp.where(column == 0, other_id, 0), second)
    return jnp.stack([first_id, second_id], axis=-1).reshape(TOKENS, 2).astype(jnp.int32)


def shard_levels(rng, dims, cuts, least, top_value):
    level = 1.0
    for dim, parts in cuts:
        heights = jax.random.uniform(jax.random.fold_in(jax.random.fold_in(rng, 6), dim), (parts,), jnp.float32, least / len(cuts), top_value / len(cuts))
        level = level * jnp.repeat(jnp.exp(heights), dims[dim] // parts).reshape((-1,) + (1,) * (len(dims) - 1 - dim))
    return level


def bell_draw(own_key, shape, deviation, bound, cuts=(), kind=jnp.bfloat16):
    result = jax.random.normal(own_key, shape, jnp.float32) * deviation
    if len(cuts) > 0:
        result = shard_levels(own_key, shape, cuts, -0.22, 0.18) * result
    return jnp.clip(result, min=-bound, max=bound).astype(kind)


def setup_inputs(seed: int = 0) -> dict:
    splits = jax.random.split(jax.random.key(seed), 8)
    return {
        "tokens": bell_draw(splits[0], (TOKENS, D), 1.0, 6.0, ((0, 64), (1, 8))),
        "expert_ids": draw_expert_ids(jax.random.fold_in(splits[7], 71), 0),
        "combine_weights": jnp.clip(0.1 + 0.9 * jax.random.uniform(splits[2], (TOKENS, 2), jnp.float32) ** shard_levels(splits[2], (TOKENS, 2), ((0, 64),), -0.2, 0.2), 0.1, 1.0),
        "grad_out": bell_draw(splits[3], (TOKENS, D), 1.0, 6.0, ((0, 64), (1, 8))),
        "gate_pre": bell_draw(splits[4], (SLOTS, FF), 1.5, 6.0, ((0, 64), (1, 8))),
        "w_up": bell_draw(splits[5], (D, FF), D ** -0.5, 0.109375, ((0, 64), (1, 8))),
        "w_down": bell_draw(splits[6], (D, FF), FF ** -0.5, 0.0625, ((0, 64), (1, 8))),
    }


def rounded(values):
    return lax.optimization_barrier(values.astype(jnp.bfloat16)).astype(jnp.float32)


def grouped_sum(hidden_rows, matrix):
    group_width = matrix.shape[1] // N_TENSOR
    summed = jnp.zeros((hidden_rows.shape[0], matrix.shape[0]), jnp.float32)
    for group_index in range(N_TENSOR):
        first_col = group_index * group_width
        part_rows = hidden_rows[:, first_col:first_col + group_width]
        part_matrix = matrix[:, first_col:first_col + group_width]
        summed = summed + rounded(jnp.dot(part_rows, part_matrix.T, preferred_element_type=jnp.float32))
    return summed


def place_rows(source, slot_index):
    holder = jnp.zeros((CAP + 1, source.shape[1]), source.dtype)
    return holder.at[slot_index].set(source)[:CAP]


def reference(tokens, expert_ids, combine_weights, grad_out, gate_pre, w_up, w_down):
    def one_group(operands):
        tok_rows, id_rows, weight_rows, grad_rows, gate_rows = operands
        chosen = id_rows == 0
        routed = jnp.any(chosen, axis=1)
        weight = jnp.sum(jnp.where(chosen, weight_rows, 0.0), axis=1)
        position = jnp.cumsum(routed.astype(jnp.int32), dtype=jnp.int32) - 1
        slot_index = jnp.where(routed, position, CAP).astype(jnp.int32)
        x_slots = place_rows(tok_rows, slot_index)
        scaled_grad = (weight[:, None] * grad_rows.astype(jnp.float32)).astype(jnp.bfloat16)
        g_slots = place_rows(scaled_grad, slot_index)
        up_value = jnp.dot(x_slots, w_up, preferred_element_type=jnp.float32)
        gate_value = gate_rows.astype(jnp.float32)
        sigmoid_gate = jax.nn.sigmoid(gate_value)
        silu_gate = gate_value * sigmoid_gate
        hidden = (silu_gate * up_value).astype(jnp.bfloat16)
        out_slots = grouped_sum(hidden, w_down)
        slot_of_token = jnp.clip(position, 0, CAP - 1).astype(jnp.int32)
        mixed = jnp.where(routed[:, None], weight[:, None] * out_slots[slot_of_token], 0.0).astype(jnp.bfloat16)
        grad_hidden = jnp.dot(g_slots, w_down, preferred_element_type=jnp.float32)
        grad_up = (grad_hidden * silu_gate).astype(jnp.bfloat16)
        grad_gate = (grad_hidden * up_value * sigmoid_gate * (1.0 + gate_value * (1.0 - sigmoid_gate))).astype(jnp.bfloat16)
        grad_slots = grouped_sum(grad_up, w_up)
        grad_tokens = jnp.where(routed[:, None], grad_slots[slot_of_token], 0.0).astype(jnp.bfloat16)
        return mixed, grad_tokens, grad_gate

    mixed, grad_tokens, grad_gate = lax.map(one_group, (tokens.reshape(N_DP, TOK_DEV, D), expert_ids.reshape(N_DP, TOK_DEV, 2), combine_weights.reshape(N_DP, TOK_DEV, 2), grad_out.reshape(N_DP, TOK_DEV, D), gate_pre.reshape(N_DP, CAP, FF)))
    return (mixed.reshape(TOKENS, D), grad_tokens.reshape(TOKENS, D), grad_gate.reshape(SLOTS, FF))
```

```python
import jax
import jax.numpy as jnp
from jax import lax
from jax.sharding import Mesh, PartitionSpec as P

DP = ("x", "z", "c")
TENSOR = ("h", "y")


def shifted(value, axis, steps):
    count = lax.axis_size(axis)
    return lax.ppermute(value, axis, [(i, (i + steps) % count) for i in range(count)])


def place_rows(source, slot_index, capacity):
    slots = lax.broadcasted_iota(jnp.int32, (capacity, source.shape[0]), 0)
    chosen = (slots == slot_index[None, :]).astype(source.dtype)
    return jnp.dot(chosen, source, preferred_element_type=jnp.float32).astype(source.dtype)


def rounded(values):
    return lax.optimization_barrier(values.astype(jnp.bfloat16))


def spread_features(part):
    other = shifted(part, "h", 1)
    h = lax.axis_index("h")
    y = lax.axis_index("y")
    low = jnp.where(h == 0, part, other)
    high = jnp.where(h == 0, other, part)
    pair = jnp.stack([low, high])
    around = {0: pair, 1: shifted(pair, "y", -1), 3: shifted(pair, "y", 1), 2: shifted(pair, "y", 2)}
    whole = jnp.zeros((2, 4) + part.shape, part.dtype)
    for offset, block in around.items():
        whole = lax.dynamic_update_slice_in_dim(whole, block[:, None], (y + offset) % 4, 1)
    whole = whole.reshape((8,) + part.shape)
    return jnp.concatenate([whole[i] for i in range(8)], axis=-1)


def partial_block(matrix, hidden_rows, y):
    width = matrix.shape[0] // 8
    view = matrix.reshape(2, 4, width, matrix.shape[1])
    block = lax.dynamic_slice_in_dim(view, y, 1, 1).reshape(2 * width, matrix.shape[1])
    value = lax.dot_general(
        block, hidden_rows, (((1,), (1,)), ((), ())), preferred_element_type=jnp.float32
    )
    return rounded(value).reshape(2, width, hidden_rows.shape[0])


def reduce_features(matrix, hidden_rows):
    h = lax.axis_index("h")
    y = lax.axis_index("y")
    arrived = [
        shifted(partial_block(matrix, hidden_rows, (y + offset) % 4), "y", offset)
        for offset in (2, 1, 3)
    ]
    total = partial_block(matrix, hidden_rows, y).astype(jnp.float32)
    for block in arrived:
        total = total + block.astype(jnp.float32)
    away = lax.dynamic_index_in_dim(total, 1 - h, 0, keepdims=False).astype(jnp.bfloat16)
    home = lax.dynamic_index_in_dim(total, h, 0, keepdims=False)
    return (home + shifted(away, "h", 1).astype(jnp.float32)).T


def on_device(tokens, expert_ids, combine_weights, grad_out, gate_pre, w_up, w_down):
    capacity = gate_pre.shape[0]
    ff = gate_pre.shape[1]
    both = lax.all_gather(jnp.concatenate([w_up, w_down], axis=1), DP, axis=0, tiled=True)
    up_full = both[:, :ff]
    down_full = both[:, ff:]
    chosen = expert_ids == 0
    routed = jnp.any(chosen, axis=1)
    weight = jnp.sum(jnp.where(chosen, combine_weights, 0.0), axis=1)
    position = jnp.cumsum(routed.astype(jnp.int32), dtype=jnp.int32) - 1
    slot_index = jnp.where(routed, position, capacity)
    scaled_grad = (weight[:, None] * grad_out.astype(jnp.float32)).astype(jnp.bfloat16)
    part = jnp.stack(
        [place_rows(tokens, slot_index, capacity), place_rows(scaled_grad, slot_index, capacity)]
    )
    spread = spread_features(part)
    x_slots = spread[0]
    g_slots = spread[1]
    up_value = jnp.dot(x_slots, up_full, preferred_element_type=jnp.float32)
    grad_hidden = jnp.dot(g_slots, down_full, preferred_element_type=jnp.float32)
    gate_value = gate_pre.astype(jnp.float32)
    sigmoid_gate = jax.nn.sigmoid(gate_value)
    silu_gate = gate_value * sigmoid_gate
    hidden = (silu_gate * up_value).astype(jnp.bfloat16)
    grad_up = (grad_hidden * silu_gate).astype(jnp.bfloat16)
    grad_gate = (
        grad_hidden * up_value * sigmoid_gate * (1.0 + gate_value * (1.0 - sigmoid_gate))
    ).astype(jnp.bfloat16)
    slot_of_token = jnp.clip(position, 0, capacity - 1)
    out_slots = reduce_features(down_full, hidden)
    mixed = jnp.where(routed[:, None], weight[:, None] * out_slots[slot_of_token], 0.0).astype(
        jnp.bfloat16
    )
    grad_slots = reduce_features(up_full, grad_up)
    grad_tokens = jnp.where(routed[:, None], grad_slots[slot_of_token], 0.0).astype(jnp.bfloat16)
    return (mixed, grad_tokens, grad_gate)


def solution(mesh):
    fine = Mesh(mesh.devices.reshape(4, 8, 2, 2, 4), DP + TENSOR)
    in_specs = (
        P(DP, TENSOR),
        P(DP, None),
        P(DP, None),
        P(DP, TENSOR),
        P(DP, TENSOR),
        P(DP, TENSOR),
        P(DP, TENSOR),
    )
    out_specs = (P(DP, TENSOR), P(DP, TENSOR), P(DP, TENSOR))
    return jax.shard_map(
        on_device, mesh=fine, in_specs=in_specs, out_specs=out_specs, check_vma=False
    )
```
